128 devices in a mesh: seq: 16 (over x, z), hx: 8 (over y, core).
Axes of the slice: x: 4, y: 4, z: 4, core: 2. Of those that a mesh axis runs over, the one named last changes fastest.
Arguments:
- query: bfloat16 [16384, 8192], P('seq', 'hx'), may hold values from -6 to 6
- key_in: bfloat16 [16384, 8192], P('seq', 'hx'), may hold values from -6 to 6
- value: bfloat16 [16384, 8192], P('seq', 'hx'), may hold values from -6 to 6
- head_gain: float32 [8192], P('hx'), may hold values from 0.1 to 1.9
- out_weight: bfloat16 [8192, 6144], P('hx', 'seq'), may hold values from -0.0625 to 0.0625
- residual: bfloat16 [16384, 6144], P(('seq', 'hx')), may hold values from -6 to 6
Outputs:
- mixed: bfloat16 [16384, 6144], P(('seq', 'hx'))
The draws below stay inside these ranges and needn't reach their ends.
All inputs are finite; a program needn't handle non-finite values.
Results may differ from the reference program's by a relative error of at most 0.014.
Values may be sent and summed in bfloat16 or wider, within the bound.
No kernel may reach another device: no remote copies, remote signals or barrier semaphores. Data moves between devices by JAX's collectives and lax.ppermute only.
A program may use at most 128 MiB of HBM per device.

```python
import jax
import jax.numpy as jnp
from jax import lax

D = 6144
HEADS = 64
DH = 128
TOK_DEV = 1024
TOKENS = 16384
HEAD_GROUPS = 8


def levels(stream_key, shape, split, low, high):
    loudness, own = 1.0, jax.random.fold_in(stream_key, 6)
    for position, shards_of in split:
        steps = jnp.exp(jax.random.uniform(jax.random.fold_in(own, position), (shards_of,), jnp.float32, low / len(split), high / len(split)))
        loudness = loudness * jnp.repeat(steps, shape[position] // shards_of).reshape([-1 if axis == position else 1 for axis in range(len(shape))])
    return loudness


def bell_draw(stream_key, extent, scale, reach, shards=(), kind=jnp.bfloat16):
    gain = levels(stream_key, extent, shards, -0.22, 0.18) if shards else 1.0
    entries = jax.random.normal(stream_key, extent, jnp.float32) * scale * gain
    return jnp.minimum(jnp.maximum(entries, -reach), reach).astype(kind)


def setup_inputs(seed: int = 0) -> dict:
    keys = jax.random.split(jax.random.key(seed), 7)
    return {
        "query": bell_draw(keys[0], (TOKENS, HEADS * DH), 1.0, 6.0, ((0, 16), (1, 8))),
        "key_in": bell_draw(keys[1], (TOKENS, HEADS * DH), 1.0, 6.0, ((0, 16), (1, 8))),
        "value": bell_draw(keys[2], (TOKENS, HEADS * DH), 1.0, 6.0, ((0, 16), (1, 8))),
        "head_gain": jnp.clip(1.0 + 0.18 * jax.random.normal(keys[3], (HEADS * DH,), jnp.float32), 0.1, 1.9),
        "out_weight": bell_draw(keys[4], (HEADS * DH, D), (HEADS * DH) ** -0.5, 0.0625, ((0, 8), (1, 16))),
        "residual": bell_draw(keys[5], (TOKENS, D), 1.0, 6.0, ((0, 128),)),
    }


def activate(array):
    return jax.nn.silu(array.astype(jnp.float32)).astype(jnp.bfloat16)

def reference(query, key_in, value, head_gain, out_weight, residual):
    q_act = activate(query)
    k_act = activate(key_in)
    blocks = min(512, TOK_DEV)
    count = TOKENS // blocks
    q_blocks = q_act.reshape(count, blocks, HEADS, DH)
    k_blocks = k_act.reshape(count, blocks, HEADS, DH)
    v_blocks = value.reshape(count, blocks, HEADS, DH)
    rows = jnp.arange(blocks, dtype=jnp.int32)
    lower = rows[:, None] >= rows[None, :]
    highest = lax.Precision.HIGHEST

    def advance(state, inputs):
        q_part, k_part, v_part = inputs
        q_full = q_part.astype(jnp.float32)
        k_full = k_part.astype(jnp.float32)
        v_full = v_part.astype(jnp.float32)
        scores = jnp.einsum('thd,shd->hts', q_full, k_full, precision=highest)
        scores = jnp.where(lower[None, :, :], scores, jnp.zeros_like(scores))
        inner = jnp.einsum('hts,she->the', scores, v_full, precision=highest)
        outer = jnp.einsum('thd,hde->the', q_full, state, precision=highest)
        state = state + jnp.einsum('thd,the->hde', k_full, v_full, precision=highest)
        return (state, inner + outer)
    start = jnp.zeros((HEADS, DH, DH), jnp.float32)
    unused, attended = lax.scan(advance, start, (q_blocks, k_blocks, v_blocks))
    attended = attended.reshape(TOKENS, HEADS, DH)
    meansq = lax.optimization_barrier(jnp.mean(attended * attended, axis=-1, keepdims=True))
    normed = attended * lax.rsqrt(meansq + 1e-06) * head_gain.reshape(HEADS, DH)
    normed = normed.astype(jnp.bfloat16).reshape(TOKENS, HEADS * DH)
    group_width = HEADS * DH // HEAD_GROUPS
    total = residual.astype(jnp.float32)
    for group in range(HEAD_GROUPS):
        lo_col = group * group_width
        part = jnp.dot(normed[:, lo_col:lo_col + group_width], out_weight[lo_col:lo_col + group_width, :], preferred_element_type=jnp.float32)
        part = lax.optimization_barrier(part.astype(jnp.bfloat16))
        total = total + part.astype(jnp.float32)
    return total.astype(jnp.bfloat16)
```

```python
import functools

import jax
import jax.numpy as jnp
from jax import lax
from jax.experimental import pallas as pl
from jax.experimental.pallas import tpu as pltpu
from jax.sharding import Mesh, PartitionSpec as P

DH = 128
F32 = jnp.float32
BF16 = jnp.bfloat16
REL = (0, 1, 3, 2)
YREL = (2, 1, 3, 0)
CHUNK = 256


def silu(block):
    wide = block.astype(F32)
    return (0.5 * wide * (1.0 + jnp.tanh(0.5 * wide))).astype(BF16)


def after(value, *others):
    return lax.optimization_barrier((value, *others))[0]


def cost(flops, moved):
    return pl.CostEstimate(flops=int(flops), transcendentals=0, bytes_accessed=int(moved))


def contract(left, right, dims):
    return lax.dot_general(left, right, (dims, ((), ())), preferred_element_type=F32)


def state_body(k_ref, v_ref, kact_ref, state_ref):
    k_act = silu(k_ref[...])
    kact_ref[...] = k_act
    both = contract(k_act, v_ref[...], ((0,), (0,))).astype(BF16)
    state_ref[:DH, :] = both[:DH, :DH]
    state_ref[DH:, :] = both[DH:, DH:]


def span_state(key_in, value):
    tokens, width = key_in.shape
    column = pl.BlockSpec((tokens, 2 * DH), lambda h: (0, h))
    return pl.pallas_call(
        state_body,
        grid=(width // (2 * DH),),
        in_specs=[column, column],
        out_specs=[column, pl.BlockSpec((2 * DH, DH), lambda h: (h, 0))],
        out_shape=[
            jax.ShapeDtypeStruct((tokens, width), BF16),
            jax.ShapeDtypeStruct((width, DH), BF16),
        ],
        cost_estimate=cost(2 * tokens * width * DH, 24e6),
        name="span_state",
    )(key_in, value)


def local_body(q_ref, kact_ref, v_ref, qact_ref, local_ref):
    q_act = silu(q_ref[...])
    qact_ref[...] = q_act
    tokens = q_act.shape[0]
    rows = lax.broadcasted_iota(jnp.int32, (CHUNK, CHUNK), 0)
    cols = lax.broadcasted_iota(jnp.int32, (CHUNK, CHUNK), 1)
    running = None
    for start in range(0, tokens, CHUNK):
        q_part = q_act[start : start + CHUNK]
        k_part = kact_ref[start : start + CHUNK, :]
        v_part = v_ref[start : start + CHUNK, :]
        scores = contract(q_part, k_part, ((1,), (1,)))
        scores = jnp.where(rows >= cols, scores, 0.0).astype(BF16)
        inner = contract(scores, v_part, ((1,), (0,)))
        if running is not None:
            inner = inner + contract(q_part, running.astype(BF16), ((1,), (0,)))
        local_ref[start : start + CHUNK, :] = inner
        if start + CHUNK < tokens:
            update = contract(k_part, v_part, ((0,), (0,)))
            running = update if running is None else running + update


def local_attention(query, k_act, value, first, heads):
    tokens, width = query.shape[0], heads * DH
    source = pl.BlockSpec((tokens, DH), lambda h: (0, h + first))
    column = pl.BlockSpec((tokens, DH), lambda h: (0, h))
    return pl.pallas_call(
        local_body,
        grid=(heads,),
        in_specs=[source, source, source],
        out_specs=[column, column],
        out_shape=[
            jax.ShapeDtypeStruct((tokens, width), BF16),
            jax.ShapeDtypeStruct((tokens, width), F32),
        ],
        cost_estimate=cost(8 * tokens * width * DH, 36e6 * width / 1024),
        name="local_attention",
    )(query, k_act, value)


def norm_body(
    tab_ref, qa_ref, la_ref, qb_ref, lb_ref, gain_ref, z1, z2, z3, x1, x2, x3, theirs_ref, mine_ref
):
    def part(q_ref, local_ref):
        prefix = x1[...].astype(F32) + x2[...].astype(F32) + x3[...].astype(F32)
        for index, piece in enumerate((z1, z2, z3)):
            prefix = prefix + jnp.where(tab_ref[8 + index] > 0, piece[...].astype(F32), 0.0)
        prefix = prefix.astype(BF16)
        zero = jnp.zeros((DH, DH), BF16)
        prefix = jnp.concatenate(
            [
                jnp.concatenate([prefix[:DH], zero], axis=1),
                jnp.concatenate([zero, prefix[DH:]], axis=1),
            ],
            axis=0,
        )
        head = lax.broadcasted_iota(jnp.int32, (2 * DH, 2 * DH), 0) // DH
        other = lax.broadcasted_iota(jnp.int32, (2 * DH, 2 * DH), 1) // DH
        average = jnp.where(head == other, 1.0 / DH, 0.0).astype(BF16)
        gain = gain_ref[...]
        for place in range(8):
            source = pl.ds(pl.multiple_of(tab_ref[place] * 128, 128), 128)
            attended = local_ref[source, :] + contract(q_ref[source, :], prefix, ((1,), (0,)))
            square = attended * attended
            high = square.astype(BF16)
            low = (square - high.astype(F32)).astype(BF16)
            meansq = contract(high, average, ((1,), (0,))) + contract(low, average, ((1,), (0,)))
            normed = (attended * lax.rsqrt(meansq + 1e-06) * gain).astype(BF16)
            out = theirs_ref if place < 4 else mine_ref
            out[(place % 4) * 128 : (place % 4 + 1) * 128, :] = normed

    early = pl.program_id(0) < pl.num_programs(0) // 2
    pl.when(early)(lambda: part(qa_ref, la_ref))
    pl.when(jnp.logical_not(early))(lambda: part(qb_ref, lb_ref))


def norm(table, halves, gain, z_pieces, x_pieces):
    (qa, la), (qb, lb) = halves
    tokens, width = qa.shape[0], qa.shape[1] * 2
    steps = width // (2 * DH)
    first = pl.BlockSpec((tokens, 2 * DH), lambda h, t: (0, jnp.minimum(h, steps // 2 - 1)))
    second = pl.BlockSpec((tokens, 2 * DH), lambda h, t: (0, jnp.maximum(h - steps // 2, 0)))
    half = pl.BlockSpec((tokens // 2, 2 * DH), lambda h, t: (0, h))
    square = pl.BlockSpec((2 * DH, DH), lambda h, t: (h, 0))
    return pl.pallas_call(
        norm_body,
        grid_spec=pltpu.PrefetchScalarGridSpec(
            num_scalar_prefetch=1,
            grid=(steps,),
            in_specs=[first, first, second, second, pl.BlockSpec((1, 2 * DH), lambda h, t: (0, h))]
            + [square] * 6,
            out_specs=[half, half],
        ),
        out_shape=[jax.ShapeDtypeStruct((tokens // 2, width), BF16)] * 2,
        cost_estimate=cost(2 * tokens * width * DH, 28e6),
        name="norm",
    )(table, qa, la, qb, lb, gain, *z_pieces, *x_pieces)


def project_body(counts, split, n_ref, *refs):
    weights = refs[: len(counts)]
    rest = refs[len(counts) :]
    step = pl.program_id(0)
    first = 0
    for w_ref, count in zip(weights, counts):

        @pl.when((step >= first) & (step < first + count))
        def _(w_ref=w_ref):
            total = contract(n_ref[...], w_ref[...], ((1,), (1,)))
            if not split:
                rest[0][...] = total.astype(BF16)
            else:
                total = total + rest[0][...].astype(F32)
                for index, out in enumerate(rest[1:]):
                    out[...] = total[index * 128 : (index + 1) * 128].astype(out.dtype)

        first += count


def project(normed, weights, tile, received=None):
    rows, depth = normed.shape
    counts = tuple(w.shape[0] // tile for w in weights)
    columns = tile * sum(counts)
    specs, first = [], 0
    for count in counts:
        specs.append(
            pl.BlockSpec(
                (tile, depth),
                lambda g, first=first, count=count: (jnp.clip(g - first, 0, count - 1), 0),
            )
        )
        first += count
    split = received is not None
    in_specs = [pl.BlockSpec((rows, depth), lambda g: (0, 0))] + specs
    args = [normed, *weights]
    if split:
        in_specs.append(pl.BlockSpec((rows, tile), lambda g: (0, g)))
        args.append(received)
        out_specs = [pl.BlockSpec((128, tile), lambda g: (0, g))] * 4
        out_shape = [jax.ShapeDtypeStruct((128, columns), BF16)] * 3 + [
            jax.ShapeDtypeStruct((128, columns), F32)
        ]
    else:
        out_specs = pl.BlockSpec((rows, tile), lambda g: (0, g))
        out_shape = jax.ShapeDtypeStruct((rows, columns), BF16)
    return pl.pallas_call(
        functools.partial(project_body, counts, split),
        grid=(sum(counts),),
        in_specs=in_specs,
        out_specs=out_specs,
        out_shape=out_shape,
        compiler_params=pltpu.CompilerParams(vmem_limit_bytes=40 * 1024 * 1024),
        cost_estimate=cost(2 * rows * depth * columns, 2 * depth * (rows + columns) + 2 * rows * columns),
        name="project",
    )(*args)


def finish_body(layout, counts, tab_ref, res_ref, *refs):
    out_ref = refs[-1]
    sums, index = [], 0
    for count in counts:
        total = refs[index][...]
        for other in refs[index + 1 : index + count]:
            total = total + other[...].astype(F32)
        sums.append(total)
        index += count
    for place, (first, second) in enumerate(layout):
        (c0, o0), (c1, o1) = first, second
        both = jnp.concatenate([sums[c0][:, o0 : o0 + 192], sums[c1][:, o1 : o1 + 192]], axis=1)
        target = pl.ds(pl.multiple_of(tab_ref[place] * 384, 128), 384)
        out_ref[:, target] = (both + res_ref[:, target].astype(F32)).astype(BF16)


def finish(layout, table, residual, parts):
    flat = [array for part in parts for array in part]
    return pl.pallas_call(
        functools.partial(finish_body, layout, tuple(len(part) for part in parts)),
        in_specs=[pl.BlockSpec(memory_space=pltpu.SMEM)]
        + [pl.BlockSpec(memory_space=pltpu.VMEM)] * (1 + len(flat)),
        out_specs=pl.BlockSpec(memory_space=pltpu.VMEM),
        out_shape=jax.ShapeDtypeStruct(residual.shape, BF16),
        compiler_params=pltpu.CompilerParams(vmem_limit_bytes=40 * 1024 * 1024),
        cost_estimate=cost(0, 12e6),
        name="finish",
    )(table, residual, *flat)


def fetch(array, axis, offset):
    return lax.ppermute(array, axis, [((i + offset) % 4, i) for i in range(4)])


def earlier(array, axis, offset):
    return lax.ppermute(array, axis, [(i, i + offset) for i in range(4 - offset)])


def swap(array):
    return lax.ppermute(array, "c", [(0, 1), (1, 0)])


def scatter_chunk(theirs, mine, a_parts, b_parts, tile, direct):
    weights = a_parts + b_parts
    a_columns = sum(w.shape[0] for w in a_parts)
    received = swap(project(theirs, weights, tile))
    far, right, left, own = project(mine, weights, tile, received)
    if direct:
        return own, fetch(right, "y", 3), fetch(left, "y", 1), fetch(far, "y", 2)
    far_right = fetch(far[:, :a_columns], "y", 3)
    far_left = fetch(far[:, a_columns:], "y", 1)
    right = jnp.concatenate(
        [(right[:, :a_columns].astype(F32) + far_right.astype(F32)).astype(BF16), right[:, a_columns:]],
        axis=1,
    )
    left = jnp.concatenate(
        [left[:, :a_columns], (left[:, a_columns:].astype(F32) + far_left.astype(F32)).astype(BF16)],
        axis=1,
    )
    return own, fetch(right, "y", 3), fetch(left, "y", 1)


def per_device(query, key_in, value, head_gain, out_weight, residual):
    x, z, y, c = (lax.axis_index(name) for name in ("x", "z", "y", "c"))
    blocks = [(y + offset) % 4 * 2 + 1 - c for offset in YREL]
    blocks += [(y + offset) % 4 * 2 + c for offset in YREL]
    flags = [((z + offset) % 4 < z).astype(jnp.int32) for offset in REL[1:]]
    table = jnp.stack([jnp.asarray(entry, jnp.int32) for entry in blocks + flags])

    turned = out_weight.T
    half = turned.shape[0] // 2
    a_own, b_own = turned[:half], turned[half:]
    a_near = [fetch(a_own, "z", offset) for offset in (1, 3)]
    b_near = [fetch(b_own, "x", offset) for offset in (1, 3)]

    k_act, state = span_state(after(key_in, turned), value)
    z_pieces = [fetch(state, "z", offset) for offset in REL[1:]]
    a_far = fetch(after(a_own, state), "z", 2)
    b_far = fetch(after(b_own, state), "x", 2)

    heads = query.shape[1] // DH // 2
    early = local_attention(query, k_act, value, 0, heads)
    z_pieces = [after(piece, early[0]) for piece in z_pieces]
    row = state.astype(F32)
    for piece in z_pieces:
        row = row + piece.astype(F32)
    row = row.astype(BF16)
    x_pieces = [earlier(row, "x", offset) for offset in (1, 2, 3)]
    late = local_attention(after(query, row), k_act, value, heads, heads)

    b0 = jnp.concatenate([b_own] + b_near + [b_far], axis=0)
    b1, b3 = fetch(b0, "z", 1), fetch(b0, "z", 3)
    a0 = jnp.concatenate([a_own] + a_near + [a_far], axis=0)
    ready = after(a0, *x_pieces)
    a1, a3 = fetch(ready, "x", 1), fetch(ready, "x", 3)
    theirs, mine = norm(table, (early, late), head_gain.reshape(1, -1), z_pieces, x_pieces)
    first = scatter_chunk(theirs, mine, [a0], [b0], 4 * half, True)
    a2 = [fetch(a1[: 2 * half], "x", 1), fetch(a3[2 * half :], "x", 3)]
    b2 = [fetch(b1[: 2 * half], "z", 1), fetch(b3[2 * half :], "z", 3)]
    second = scatter_chunk(after(theirs, first[0]), mine, [a1, a3], [b1, b3], 4 * half, False)
    third = scatter_chunk(after(theirs, second[0]), mine, a2, b2, 2 * half, True)
    parts = [first, second, third]
    a_group = ((0, 0), (1, 0), (1, 4 * half), (2, 0))
    b_group = ((0, 4 * half), (1, 8 * half), (1, 12 * half), (2, 4 * half))
    layout, shards = [], []
    for i, x_off in enumerate(REL):
        for j, z_off in enumerate(REL):
            layout.append(
                (
                    (a_group[i][0], a_group[i][1] + j * half),
                    (b_group[j][0], b_group[j][1] + i * half),
                )
            )
            shards.append((x + x_off) % 4 * 4 + (z + z_off) % 4)
    shard_table = jnp.stack([jnp.asarray(entry, jnp.int32) for entry in shards])
    return finish(tuple(layout), shard_table, residual, parts)


def solution(mesh):
    torus = Mesh(mesh.devices.reshape(4, 4, 4, 2), ("x", "z", "y", "c"))
    seq, hx = ("x", "z"), ("y", "c")
    return jax.shard_map(
        per_device,
        mesh=torus,
        in_specs=(P(seq, hx), P(seq, hx), P(seq, hx), P(hx), P(hx, seq), P(seq + hx, None)),
        out_specs=P(seq + hx, None),
        check_vma=False,
    )
```

```python
import functools

import jax
import jax.numpy as jnp
from jax import lax
from jax.experimental import pallas as pl
from jax.experimental.pallas import tpu as pltpu
from jax.sharding import Mesh, PartitionSpec as P

DH = 128
F32 = jnp.float32
BF16 = jnp.bfloat16
REL = (0, 1, 3, 2)
YREL = (2, 1, 3, 0)
CHUNK = 256


def silu(block):
    wide = block.astype(F32)
    return (0.5 * wide * (1.0 + jnp.tanh(0.5 * wide))).astype(BF16)


def after(value, *others):
    return lax.optimization_barrier((value, *others))[0]


def contract(left, right, dims):
    return lax.dot_general(left, right, (dims, ((), ())), preferred_element_type=F32)


def state_body(k_ref, v_ref, kact_ref, state_ref):
    k_act = silu(k_ref[...])
    kact_ref[...] = k_act
    both = contract(k_act, v_ref[...], ((0,), (0,))).astype(BF16)
    state_ref[:DH, :] = both[:DH, :DH]
    state_ref[DH:, :] = both[DH:, DH:]


def span_state(key_in, value):
    tokens, width = key_in.shape
    column = pl.BlockSpec((tokens, 2 * DH), lambda h: (0, h))
    return pl.pallas_call(
        state_body,
        grid=(width // (2 * DH),),
        in_specs=[column, column],
        out_specs=[column, pl.BlockSpec((2 * DH, DH), lambda h: (h, 0))],
        out_shape=[
            jax.ShapeDtypeStruct((tokens, width), BF16),
            jax.ShapeDtypeStruct((width, DH), BF16),
        ],
        name="span_state",
    )(key_in, value)


def local_body(q_ref, kact_ref, v_ref, qact_ref, local_ref):
    q_act = silu(q_ref[...])
    qact_ref[...] = q_act
    tokens = q_act.shape[0]
    rows = lax.broadcasted_iota(jnp.int32, (CHUNK, CHUNK), 0)
    cols = lax.broadcasted_iota(jnp.int32, (CHUNK, CHUNK), 1)
    running = None
    for start in range(0, tokens, CHUNK):
        q_part = q_act[start : start + CHUNK]
        k_part = kact_ref[start : start + CHUNK, :]
        v_part = v_ref[start : start + CHUNK, :]
        scores = contract(q_part, k_part, ((1,), (1,)))
        scores = jnp.where(rows >= cols, scores, 0.0).astype(BF16)
        inner = contract(scores, v_part, ((1,), (0,)))
        if running is not None:
            inner = inner + contract(q_part, running.astype(BF16), ((1,), (0,)))
        local_ref[start : start + CHUNK, :] = inner
        if start + CHUNK < tokens:
            update = contract(k_part, v_part, ((0,), (0,)))
            running = update if running is None else running + update


def local_attention(query, k_act, value, first, heads):
    tokens, width = query.shape[0], heads * DH
    source = pl.BlockSpec((tokens, DH), lambda h: (0, h + first))
    column = pl.BlockSpec((tokens, DH), lambda h: (0, h))
    return pl.pallas_call(
        local_body,
        grid=(heads,),
        in_specs=[source, source, source],
        out_specs=[column, column],
        out_shape=[
            jax.ShapeDtypeStruct((tokens, width), BF16),
            jax.ShapeDtypeStruct((tokens, width), F32),
        ],
        name="local_attention",
    )(query, k_act, value)


def message_body(tab_ref, state_ref, z1, z2, z3, *outs):
    pieces = [piece[...].astype(F32) for piece in (z1, z2, z3)]
    zero = jnp.zeros_like(pieces[0])
    lower = zero
    for index, piece in enumerate(pieces):
        lower = lower + jnp.where(tab_ref[8 + index] > 0, piece, zero)
    first_core = tab_ref[14] == 0
    through = jnp.where(first_core, zero, lower)
    total = state_ref[...].astype(F32)
    total = total + jnp.where(first_core, pieces[0] + pieces[1] + pieces[2], zero)
    for index, out in enumerate(outs):
        out[...] = (through + jnp.where(tab_ref[11 + index] > 0, total, zero)).astype(BF16)


def messages(table, state, pieces):
    whole = pl.BlockSpec(state.shape, lambda g, t: (0, 0))
    return pl.pallas_call(
        message_body,
        grid_spec=pltpu.PrefetchScalarGridSpec(
            num_scalar_prefetch=1, grid=(1,), in_specs=[whole] * 4, out_specs=[whole] * 3
        ),
        out_shape=[jax.ShapeDtypeStruct(state.shape, BF16)] * 3,
        name="messages",
    )(table, state, *pieces)


def norm_body(
    tab_ref, qa_ref, la_ref, qb_ref, lb_ref, gain_ref, z1, z2, z3, x1, x2, x3, out_ref
):
    def part(q_ref, local_ref):
        prefix = x1[...].astype(F32) + x2[...].astype(F32) + x3[...].astype(F32)
        for index, piece in enumerate((z1, z2, z3)):
            prefix = prefix + jnp.where(tab_ref[8 + index] > 0, piece[...].astype(F32), 0.0)
        prefix = prefix.astype(BF16)
        zero = jnp.zeros((DH, DH), BF16)
        prefix = jnp.concatenate(
            [
                jnp.concatenate([prefix[:DH], zero], axis=1),
                jnp.concatenate([zero, prefix[DH:]], axis=1),
            ],
            axis=0,
        )
        head = lax.broadcasted_iota(jnp.int32, (2 * DH, 2 * DH), 0) // DH
        other = lax.broadcasted_iota(jnp.int32, (2 * DH, 2 * DH), 1) // DH
        average = jnp.where(head == other, 1.0 / DH, 0.0).astype(BF16)
        gain = gain_ref[...]
        for place in range(8):
            source = pl.ds(pl.multiple_of(tab_ref[place] * 128, 128), 128)
            attended = local_ref[source, :] + contract(q_ref[source, :], prefix, ((1,), (0,)))
            meansq = contract((attended * attended).astype(BF16), average, ((1,), (0,)))
            normed = (attended * lax.rsqrt(meansq + 1e-06) * gain).astype(BF16)
            out_ref[place * 128 : (place + 1) * 128, :] = normed

    early = pl.program_id(0) < pl.num_programs(0) // 2
    pl.when(early)(lambda: part(qa_ref, la_ref))
    pl.when(jnp.logical_not(early))(lambda: part(qb_ref, lb_ref))


def norm(table, halves, gain, z_pieces, x_pieces):
    (qa, la), (qb, lb) = halves
    tokens, width = qa.shape[0], qa.shape[1] * 2
    steps = width // (2 * DH)
    first = pl.BlockSpec((tokens, 2 * DH), lambda h, t: (0, jnp.minimum(h, steps // 2 - 1)))
    second = pl.BlockSpec((tokens, 2 * DH), lambda h, t: (0, jnp.maximum(h - steps // 2, 0)))
    pair = pl.BlockSpec((tokens, 2 * DH), lambda h, t: (0, h))
    square = pl.BlockSpec((2 * DH, DH), lambda h, t: (h, 0))
    return pl.pallas_call(
        norm_body,
        grid_spec=pltpu.PrefetchScalarGridSpec(
            num_scalar_prefetch=1,
            grid=(steps,),
            in_specs=[first, first, second, second, pl.BlockSpec((1, 2 * DH), lambda h, t: (0, h))]
            + [square] * 6,
            out_specs=pair,
        ),
        out_shape=jax.ShapeDtypeStruct((tokens, width), BF16),
        name="norm",
    )(table, qa, la, qb, lb, gain, *z_pieces, *x_pieces)


def project_body(counts, core_ref, own_ref, other_ref, *refs):
    weights, outs = refs[: len(counts)], refs[len(counts) :]
    step = pl.program_id(0)
    depth, rows = own_ref.shape[1], outs[0].shape[0]
    first_core = core_ref[0] == 0
    first = 0
    for w_ref, count in zip(weights, counts):

        @pl.when((step >= first) & (step < first + count))
        def _(w_ref=w_ref):
            total = contract(own_ref[...], w_ref[:, :depth], ((1,), (1,)))
            total = total + contract(other_ref[...], w_ref[:, depth:], ((1,), (1,)))
            far, right, left, own = (
                total[index * rows : (index + 1) * rows].astype(BF16) for index in range(4)
            )
            for out, block in zip(
                outs,
                (jnp.where(first_core, left, right), far, jnp.where(first_core, right, left), own),
            ):
                out[...] = block

        first += count


def project(core, own, other, weights, tile):
    rows, depth = own.shape
    counts = tuple(w.shape[0] // tile for w in weights)
    columns = tile * sum(counts)
    specs, first = [], 0
    for count in counts:
        specs.append(
            pl.BlockSpec(
                (tile, 2 * depth),
                lambda g, t, first=first, count=count: (jnp.clip(g - first, 0, count - 1), 0),
            )
        )
        first += count
    whole = pl.BlockSpec((rows, depth), lambda g, t: (0, 0))
    return pl.pallas_call(
        functools.partial(project_body, counts),
        grid_spec=pltpu.PrefetchScalarGridSpec(
            num_scalar_prefetch=1,
            grid=(sum(counts),),
            in_specs=[whole, whole] + specs,
            out_specs=[pl.BlockSpec((rows // 4, tile), lambda g, t: (0, g))] * 4,
        ),
        out_shape=[jax.ShapeDtypeStruct((rows // 4, columns), BF16)] * 4,
        compiler_params=pltpu.CompilerParams(vmem_limit_bytes=40 * 1024 * 1024),
        name="project",
    )(core, own, other, *weights)


def finish_body(layout, tab_ref, res_ref, *refs):
    out_ref = refs[-1]
    kept, got = refs[: len(refs) // 2], refs[len(refs) // 2 : -1]
    first_core = tab_ref[16] == 0
    groups = []
    for keep, receive in zip(kept, got):
        mine, theirs = keep[...], receive[...].astype(F32)
        groups.append((jnp.where(first_core, mine, theirs), jnp.where(first_core, theirs, mine)))
    for place, ((c0, o0), (c1, o1)) in enumerate(layout):
        both = jnp.concatenate(
            [groups[c0][0][:, o0 : o0 + 192], groups[c1][1][:, o1 : o1 + 192]], axis=1
        )
        target = pl.ds(pl.multiple_of(tab_ref[place] * 384, 128), 384)
        out_ref[:, target] = (both + res_ref[:, target].astype(F32)).astype(BF16)


def finish(layout, table, residual, kept, got):
    return pl.pallas_call(
        functools.partial(finish_body, layout),
        in_specs=[pl.BlockSpec(memory_space=pltpu.SMEM)]
        + [pl.BlockSpec(memory_space=pltpu.VMEM)] * (1 + len(kept) + len(got)),
        out_specs=pl.BlockSpec(memory_space=pltpu.VMEM),
        out_shape=jax.ShapeDtypeStruct(residual.shape, BF16),
        compiler_params=pltpu.CompilerParams(vmem_limit_bytes=40 * 1024 * 1024),
        name="finish",
    )(table, residual, *kept, *got)


def fetch(array, axis, offset):
    return lax.ppermute(array, axis, [((i + offset) % 4, i) for i in range(4)])


def fetch_mixed(array, level, offset):
    pairs = []
    for x in range(4):
        for z in range(4):
            for c in range(2):
                if (level == 1) == (c == 0):
                    source = (x, (z + offset) % 4, c)
                else:
                    source = ((x + offset) % 4, z, c)
                pairs.append(((source[0] * 4 + source[1]) * 2 + c, (x * 4 + z) * 2 + c))
    return lax.ppermute(array, ("x", "z", "c"), pairs)


def swap(array):
    return lax.ppermute(array, "c", [(0, 1), (1, 0)])


def push(array, hops):
    pairs = []
    for y in range(4):
        pairs.append((y * 2, (y + hops) % 4 * 2))
        pairs.append((y * 2 + 1, (y - hops) % 4 * 2 + 1))
    return lax.ppermute(array, ("y", "c"), pairs)


def add(left, right):
    return (left.astype(F32) + right.astype(F32)).astype(BF16)


def reduce_ring(parts):
    behind, far, ahead, own = parts
    return own, push(add(push(add(push(behind, 1), far), 1), ahead), 1)


def reduce_direct(parts):
    behind, far, ahead, own = parts
    return own, push(far, 2), push(ahead, 1), push(behind, 3)


def settle_chunk(parts, c):
    def rows(which):
        total = 0.0
        for part in parts:
            total = total + lax.dynamic_slice_in_dim(part, which * 128, 128).astype(F32)
        return total

    return rows(c), swap(rows(1 - c).astype(BF16))


def per_device(query, key_in, value, head_gain, out_weight, residual):
    x, z, y, c = (lax.axis_index(name) for name in ("x", "z", "y", "c"))
    near, away = jnp.where(c == 0, z, x), jnp.where(c == 0, x, z)
    blocks = [(y + offset) % 4 * 2 + core for offset in YREL for core in (0, 1)]
    flags = [(near + offset) % 4 < near for offset in REL[1:]]
    flags += [away < (away - offset) % 4 for offset in REL[1:]]
    table = jnp.stack([jnp.asarray(entry, jnp.int32) for entry in blocks + flags + [c]])

    turned = out_weight.T
    half = turned.shape[0] // 2
    keep = lax.dynamic_slice_in_dim(turned, c * half, half)
    give = lax.dynamic_slice_in_dim(turned, (1 - c) * half, half)
    k_act, state = span_state(after(key_in, keep, give), value)
    level1 = [fetch_mixed(state, 1, offset) for offset in REL[1:]]
    base = jnp.concatenate([keep, after(swap(give), state)], axis=1)
    near_plus, near_minus = fetch_mixed(base, 1, 1), fetch_mixed(base, 1, 3)

    heads = query.shape[1] // DH // 2
    early = local_attention(query, k_act, value, 0, heads)
    level1 = [after(piece, early[0]) for piece in level1]
    sent = messages(table, state, level1)
    level2 = [fetch_mixed(piece, 2, offset) for piece, offset in zip(sent, REL[1:])]
    far_weights = fetch_mixed(after(base, sent[0]), 1, 2)
    late = local_attention(after(query, sent[0]), k_act, value, heads, heads)
    level2 = [after(piece, late[0]) for piece in level2]

    g0a = jnp.concatenate([base, near_plus], axis=0)
    ready = after(g0a, *level2)
    g1a, g3a = fetch_mixed(ready, 2, 1), fetch_mixed(ready, 2, 3)
    table = after(table, far_weights, near_plus, near_minus)
    normed = norm(table, (early, late), head_gain.reshape(1, -1), level1, level2)
    other = swap(normed)
    g0b = jnp.concatenate([near_minus, far_weights], axis=0)
    core = c.astype(jnp.int32).reshape(1)
    first = project(core, normed, other, [g0a, g0b], 384)
    ready = after(g0b, g1a, g3a, first[0])
    g1b, g3b = fetch_mixed(ready, 2, 1), fetch_mixed(ready, 2, 3)
    first = reduce_ring(first)
    second = project(core, after(normed, first[0]), other, [g1a, g3a], 384)
    g2 = [
        fetch_mixed(after(g1a, g1b, g3b, second[0]), 2, 1),
        fetch_mixed(after(g3b, g1b, second[0]), 2, 3),
    ]
    second = reduce_ring(second)
    third = project(core, after(normed, second[0], *first), other, [g1b, g3b], 384)
    third = reduce_ring(third)
    fourth = project(core, after(normed, third[0], *second), other, g2, 384)
    fourth = reduce_direct(fourth)
    settled = [settle_chunk(parts, c) for parts in (first, second, third, fourth)]
    spot = (
        ((0, 0), (0, 1), (0, 2), (0, 3)),
        ((1, 0), (1, 1), (2, 0), (2, 1)),
        ((1, 2), (1, 3), (2, 2), (2, 3)),
        ((3, 0), (3, 1), (3, 2), (3, 3)),
    )
    layout, shards = [], []
    for i, x_off in enumerate(REL):
        for j, z_off in enumerate(REL):
            layout.append(
                tuple((chunk, part * half) for chunk, part in (spot[i][j], spot[j][i]))
            )
            shards.append((x + x_off) % 4 * 4 + (z + z_off) % 4)
    shard_table = jnp.stack([jnp.asarray(entry, jnp.int32) for entry in shards + [c]])
    kept, got = zip(*settled)
    return finish(tuple(layout), shard_table, residual, kept, got)


def solution(mesh):
    torus = Mesh(mesh.devices.reshape(4, 4, 4, 2), ("x", "z", "y", "c"))
    seq, hx = ("x", "z"), ("y", "c")
    return jax.shard_map(
        per_device,
        mesh=torus,
        in_specs=(P(seq, hx), P(seq, hx), P(seq, hx), P(hx), P(hx, seq), P(seq + hx, None)),
        out_specs=P(seq + hx, None),
        check_vma=False,
    )
```

```python
import functools

import jax
import jax.numpy as jnp
from jax import lax
from jax.experimental import pallas as pl
from jax.experimental.pallas import tpu as pltpu
from jax.sharding import Mesh, PartitionSpec as P

DH = 128
F32 = jnp.float32
BF16 = jnp.bfloat16
REL = (0, 1, 3, 2)
YREL = (2, 1, 3, 0)
CHUNK = 256


def silu(block):
    wide = block.astype(F32)
    return (0.5 * wide * (1.0 + jnp.tanh(0.5 * wide))).astype(BF16)


def after(value, *others):
    return lax.optimization_barrier((value, *others))[0]


def contract(left, right, dims):
    return lax.dot_general(left, right, (dims, ((), ())), preferred_element_type=F32)


def state_body(k_ref, v_ref, kact_ref, state_ref):
    k_act = silu(k_ref[...])
    kact_ref[...] = k_act
    both = contract(k_act, v_ref[...], ((0,), (0,))).astype(BF16)
    for head in range(2):
        square = both[head * DH : (head + 1) * DH, head * DH : (head + 1) * DH]
        for part in range(2):
            column = (2 * head + part) * DH
            state_ref[:, column : column + DH] = square[part * 64 : (part + 1) * 64]


def span_state(key_in, value):
    tokens, width = key_in.shape
    column = pl.BlockSpec((tokens, 2 * DH), lambda h: (0, h))
    return pl.pallas_call(
        state_body,
        grid=(width // (2 * DH),),
        in_specs=[column, column],
        out_specs=[column, pl.BlockSpec((64, 4 * DH), lambda h: (0, h))],
        out_shape=[
            jax.ShapeDtypeStruct((tokens, width), BF16),
            jax.ShapeDtypeStruct((64, 2 * width), BF16),
        ],
        name="span_state",
    )(key_in, value)


def local_body(q_ref, kact_ref, v_ref, qact_ref, local_ref):
    q_act = silu(q_ref[...])
    qact_ref[...] = q_act
    tokens = q_act.shape[0]
    rows = lax.broadcasted_iota(jnp.int32, (CHUNK, CHUNK), 0)
    cols = lax.broadcasted_iota(jnp.int32, (CHUNK, CHUNK), 1)
    running = None
    for start in range(0, tokens, CHUNK):
        q_part = q_act[start : start + CHUNK]
        k_part = kact_ref[start : start + CHUNK, :]
        v_part = v_ref[start : start + CHUNK, :]
        scores = contract(q_part, k_part, ((1,), (1,)))
        scores = jnp.where(rows >= cols, scores, 0.0).astype(BF16)
        inner = contract(scores, v_part, ((1,), (0,)))
        if running is not None:
            inner = inner + contract(q_part, running.astype(BF16), ((1,), (0,)))
        local_ref[start : start + CHUNK, :] = inner
        if start + CHUNK < tokens:
            update = contract(k_part, v_part, ((0,), (0,)))
            running = update if running is None else running + update


def local_attention(query, k_act, value, first, heads):
    tokens, width = query.shape[0], heads * DH
    source = pl.BlockSpec((tokens, DH), lambda h: (0, h + first))
    column = pl.BlockSpec((tokens, DH), lambda h: (0, h))
    return pl.pallas_call(
        local_body,
        grid=(heads,),
        in_specs=[source, source, source],
        out_specs=[column, column],
        out_shape=[
            jax.ShapeDtypeStruct((tokens, width), BF16),
            jax.ShapeDtypeStruct((tokens, width), F32),
        ],
        name="local_attention",
    )(query, k_act, value)


def message_body(tab_ref, state_ref, z1, z2, z3, *outs):
    pieces = [piece[...].astype(F32) for piece in (z1, z2, z3)]
    zero = jnp.zeros_like(pieces[0])
    lower = zero
    for index, piece in enumerate(pieces):
        lower = lower + jnp.where(tab_ref[8 + index] > 0, piece, zero)
    first_core = tab_ref[14] == 0
    through = jnp.where(first_core, zero, lower)
    total = state_ref[...].astype(F32)
    total = total + jnp.where(first_core, pieces[0] + pieces[1] + pieces[2], zero)
    for index, out in enumerate(outs):
        out[...] = (through + jnp.where(tab_ref[11 + index] > 0, total, zero)).astype(BF16)


def messages(table, state, pieces):
    rows, columns = state.shape
    own = pl.BlockSpec((rows, columns // 2), lambda g, t: (0, g))
    last = pl.BlockSpec((rows, columns // 2), lambda g, t: (0, g))
    return pl.pallas_call(
        message_body,
        grid_spec=pltpu.PrefetchScalarGridSpec(
            num_scalar_prefetch=1, grid=(2,), in_specs=[own] + [last] * 3, out_specs=[own] * 3
        ),
        out_shape=[jax.ShapeDtypeStruct(state.shape, BF16)] * 3,
        name="messages",
    )(table, state, *pieces)


def norm_body(
    tab_ref, q_ref, local_ref, gain_ref, z1, z2, z3, x1, x2, x3, out_ref
):
    prefix = x1[...].astype(F32) + x2[...].astype(F32) + x3[...].astype(F32)
    for index, piece in enumerate((z1, z2, z3)):
        prefix = prefix + jnp.where(tab_ref[8 + index] > 0, piece[...].astype(F32), 0.0)
    prefix = prefix.astype(BF16)
    zero = jnp.zeros((64, DH), BF16)
    strips = [prefix[:, index * DH : (index + 1) * DH] for index in range(4)]
    prefix = jnp.concatenate(
        [jnp.concatenate([strip, zero], axis=1) for strip in strips[:2]]
        + [jnp.concatenate([zero, strip], axis=1) for strip in strips[2:]],
        axis=0,
    )
    head = lax.broadcasted_iota(jnp.int32, (2 * DH, 2 * DH), 0) // DH
    other = lax.broadcasted_iota(jnp.int32, (2 * DH, 2 * DH), 1) // DH
    average = jnp.where(head == other, 1.0 / DH, 0.0).astype(BF16)
    gain = gain_ref[...]
    for place in range(8):
        source = pl.ds(pl.multiple_of(tab_ref[place] * 128, 128), 128)
        attended = local_ref[source, :] + contract(q_ref[source, :], prefix, ((1,), (0,)))
        meansq = contract((attended * attended).astype(BF16), average, ((1,), (0,)))
        normed = (attended * lax.rsqrt(meansq + 1e-06) * gain).astype(BF16)
        out_ref[place * 128 : (place + 1) * 128, :] = normed


def norm(table, half, first, gain, z_pieces, x_pieces):
    tokens, width = half[0].shape
    skip = first * DH // (2 * DH)
    pair = pl.BlockSpec((tokens, 2 * DH), lambda h, t: (0, h))
    last = pl.BlockSpec((64, 4 * DH), lambda h, t: (0, h + skip))
    square = pl.BlockSpec((64, 4 * DH), lambda h, t: (0, h + skip))
    return pl.pallas_call(
        norm_body,
        grid_spec=pltpu.PrefetchScalarGridSpec(
            num_scalar_prefetch=1,
            grid=(width // (2 * DH),),
            in_specs=[pair, pair, pl.BlockSpec((1, 2 * DH), lambda h, t: (0, h + skip))]
            + [last] * 3
            + [square] * 3,
            out_specs=pair,
        ),
        out_shape=jax.ShapeDtypeStruct((tokens, width), BF16),
        name="norm",
    )(table, *half, gain, *z_pieces, *x_pieces)


def project_body(counts, core_ref, *refs):
    tokens, weights, outs = refs[:4], refs[4 : 4 + len(counts)], refs[4 + len(counts) :]
    step = pl.program_id(0)
    depth, rows = tokens[0].shape[1], outs[0].shape[0]
    first_core = core_ref[0] == 0
    first = 0
    for w_ref, count in zip(weights, counts):

        @pl.when((step >= first) & (step < first + count))
        def _(w_ref=w_ref):
            total = 0.0
            for index, t_ref in enumerate(tokens):
                columns = slice(index * depth, (index + 1) * depth)
                total = total + contract(t_ref[...], w_ref[:, columns], ((1,), (1,)))
            far, right, left, own = (
                total[index * rows : (index + 1) * rows].astype(BF16) for index in range(4)
            )
            for out, block in zip(
                outs,
                (jnp.where(first_core, left, right), far, jnp.where(first_core, right, left), own),
            ):
                out[...] = block

        first += count


def project(core, tokens, weights, tile):
    rows, depth = tokens[0].shape
    counts = tuple(w.shape[0] // tile for w in weights)
    columns = tile * sum(counts)
    specs, first = [], 0
    for count in counts:
        specs.append(
            pl.BlockSpec(
                (tile, 4 * depth),
                lambda g, t, first=first, count=count: (jnp.clip(g - first, 0, count - 1), 0),
            )
        )
        first += count
    whole = pl.BlockSpec((rows, depth), lambda g, t: (0, 0))
    return pl.pallas_call(
        functools.partial(project_body, counts),
        grid_spec=pltpu.PrefetchScalarGridSpec(
            num_scalar_prefetch=1,
            grid=(sum(counts),),
            in_specs=[whole] * 4 + specs,
            out_specs=[pl.BlockSpec((rows // 4, tile), lambda g, t: (0, g))] * 4,
        ),
        out_shape=[jax.ShapeDtypeStruct((rows // 4, columns), BF16)] * 4,
        compiler_params=pltpu.CompilerParams(vmem_limit_bytes=40 * 1024 * 1024),
        name="project",
    )(core, *tokens, *weights)


def finish_body(layout, tab_ref, res_ref, *refs):
    out_ref = refs[-1]
    kept, got = refs[: len(refs) // 2], refs[len(refs) // 2 : -1]
    first_core = tab_ref[16] == 0
    groups = []
    for keep, receive in zip(kept, got):
        mine, theirs = keep[...], receive[...].astype(F32)
        groups.append((jnp.where(first_core, mine, theirs), jnp.where(first_core, theirs, mine)))
    for place, ((c0, o0), (c1, o1)) in enumerate(layout):
        both = jnp.concatenate(
            [groups[c0][0][:, o0 : o0 + 192], groups[c1][1][:, o1 : o1 + 192]], axis=1
        )
        target = pl.ds(pl.multiple_of(tab_ref[place] * 384, 128), 384)
        out_ref[:, target] = (both + res_ref[:, target].astype(F32)).astype(BF16)


def finish(layout, table, residual, kept, got):
    return pl.pallas_call(
        functools.partial(finish_body, layout),
        in_specs=[pl.BlockSpec(memory_space=pltpu.SMEM)]
        + [pl.BlockSpec(memory_space=pltpu.VMEM)] * (1 + len(kept) + len(got)),
        out_specs=pl.BlockSpec(memory_space=pltpu.VMEM),
        out_shape=jax.ShapeDtypeStruct(residual.shape, BF16),
        compiler_params=pltpu.CompilerParams(vmem_limit_bytes=40 * 1024 * 1024),
        name="finish",
    )(table, residual, *kept, *got)


def fetch(array, axis, offset):
    return lax.ppermute(array, axis, [((i + offset) % 4, i) for i in range(4)])


def fetch_mixed(array, level, offset):
    pairs = []
    for x in range(4):
        for z in range(4):
            for c in range(2):
                if (level == 1) == (c == 0):
                    source = (x, (z + offset) % 4, c)
                else:
                    source = ((x + offset) % 4, z, c)
                pairs.append(((source[0] * 4 + source[1]) * 2 + c, (x * 4 + z) * 2 + c))
    return lax.ppermute(array, ("x", "z", "c"), pairs)


def swap(array):
    return lax.ppermute(array, "c", [(0, 1), (1, 0)])


def push(array, hops):
    pairs = []
    for y in range(4):
        pairs.append((y * 2, (y + hops) % 4 * 2))
        pairs.append((y * 2 + 1, (y - hops) % 4 * 2 + 1))
    return lax.ppermute(array, ("y", "c"), pairs)


def add(left, right):
    return (left.astype(F32) + right.astype(F32)).astype(BF16)


def settle_chunk(parts, c):
    def rows(which):
        total = 0.0
        for part in parts:
            total = total + lax.dynamic_slice_in_dim(part, which * 128, 128).astype(F32)
        return total

    return rows(c), swap(rows(1 - c).astype(BF16))


def per_device(query, key_in, value, head_gain, out_weight, residual):
    x, z, y, c = (lax.axis_index(name) for name in ("x", "z", "y", "c"))
    near, away = jnp.where(c == 0, z, x), jnp.where(c == 0, x, z)
    blocks = [(y + offset) % 4 * 2 + core for offset in YREL for core in (0, 1)]
    flags = [(near + offset) % 4 < near for offset in REL[1:]]
    flags += [away < (away - offset) % 4 for offset in REL[1:]]
    table = jnp.stack([jnp.asarray(entry, jnp.int32) for entry in blocks + flags + [c]])

    turned = out_weight.T
    half = turned.shape[0] // 2
    keep = lax.dynamic_slice_in_dim(turned, c * half, half)
    give = lax.dynamic_slice_in_dim(turned, (1 - c) * half, half)
    k_act, state = span_state(after(key_in, keep, give), value)
    base = jnp.concatenate([keep, after(swap(give), state)], axis=1)
    level1 = [fetch_mixed(state, 1, offset) for offset in REL[1:]]
    plus, minus = fetch_mixed(base, 1, 1), fetch_mixed(base, 1, 3)

    width = query.shape[1] // 2
    heads = width // DH
    early = local_attention(query, k_act, value, 0, heads)
    level1 = [after(piece, early[0], plus, minus) for piece in level1]
    sent = messages(table, state, level1)
    level2 = [fetch_mixed(piece, 2, offset) for piece, offset in zip(sent, REL[1:])]
    far = fetch_mixed(after(base, sent[0]), 1, 2)
    late = local_attention(after(query, sent[0]), k_act, value, heads, heads)
    level2 = [after(piece, late[0]) for piece in level2]
    g0a = jnp.concatenate([base, plus], axis=0)
    g0a = after(g0a, *level2)
    g1a, g3a = fetch_mixed(g0a, 2, 1), fetch_mixed(g0a, 2, 3)
    g0b = jnp.concatenate([minus, far], axis=0)

    gain = head_gain.reshape(1, -1)
    table = after(table, far)
    norm_a = norm(table, early, 0, gain, level1, level2)
    swap_a = swap(norm_a)
    norm_b = norm(after(table, norm_a), late, heads, gain, level1, level2)
    swap_b = swap(norm_b)
    core = c.astype(jnp.int32).reshape(1)
    ready = after(g0b, g1a, g3a)
    g1b, g3b = fetch_mixed(ready, 2, 1), fetch_mixed(ready, 2, 3)

    def columns(weights, *others):
        return project(core, [after(norm_a, *others), norm_b, swap_a, swap_b], weights, 384)

    first = columns([g1a, g3a], norm_b)
    second = columns([g0a, g0b], first[0])
    first1 = push(first[0], 1)
    second1 = push(after(second[0], first1), 1)
    first2 = push(after(add(first1, first[1]), second[0]), 1)
    g2 = [
        fetch_mixed(after(g1a, g1b, g3b, second[0], first1), 2, 1),
        fetch_mixed(after(g3b, g1b, second[0], first1), 2, 3),
    ]
    second2 = push(add(second1, second[1]), 1)
    third = columns([g1b, g3b], second[0], first1)
    third1 = push(after(third[0], first2), 1)
    first3 = push(add(first2, first[2]), 1)
    second3 = push(add(second2, second[2]), 1)
    third2 = push(add(third1, third[1]), 1)
    third3 = push(add(third2, third[2]), 1)
    fourth = columns(g2, third[0], first2, second2)
    chunks = (
        (first[3], first3),
        (second[3], second3),
        (third[3], third3),
        (fourth[3], push(fourth[1], 2), push(fourth[2], 1), push(fourth[0], 3)),
    )
    settled = [settle_chunk(parts, c) for parts in chunks]
    spot = (
        ((1, 0), (1, 1), (1, 2), (1, 3)),
        ((0, 0), (0, 1), (2, 0), (2, 1)),
        ((0, 2), (0, 3), (2, 2), (2, 3)),
        ((3, 0), (3, 1), (3, 2), (3, 3)),
    )
    layout, shards = [], []
    for i, x_off in enumerate(REL):
        for j, z_off in enumerate(REL):
            layout.append(
                tuple((chunk, part * half) for chunk, part in (spot[i][j], spot[j][i]))
            )
            shards.append((x + x_off) % 4 * 4 + (z + z_off) % 4)
    shard_table = jnp.stack([jnp.asarray(entry, jnp.int32) for entry in shards + [c]])
    kept, got = zip(*settled)
    return finish(tuple(layout), shard_table, residual, kept, got)


def solution(mesh):
    torus = Mesh(mesh.devices.reshape(4, 4, 4, 2), ("x", "z", "y", "c"))
    seq, hx = ("x", "z"), ("y", "c")
    return jax.shard_map(
        per_device,
        mesh=torus,
        in_specs=(P(seq, hx), P(seq, hx), P(seq, hx), P(hx), P(hx, seq), P(seq + hx, None)),
        out_specs=P(seq + hx, None),
        check_vma=False,
    )
```

```python
import functools

import jax
import jax.numpy as jnp
from jax import lax
from jax.experimental import pallas as pl
from jax.experimental.pallas import tpu as pltpu
from jax.sharding import Mesh, PartitionSpec as P

DH = 128
F32 = jnp.float32
BF16 = jnp.bfloat16
REL = (0, 1, 3, 2)
YREL = (2, 1, 3, 0)
CHUNK = 256


def silu(block):
    wide = block.astype(F32)
    return (0.5 * wide * (1.0 + jnp.tanh(0.5 * wide))).astype(BF16)


def after(value, *others):
    return lax.optimization_barrier((value, *others))[0]


def contract(left, right, dims):
    return lax.dot_general(left, right, (dims, ((), ())), preferred_element_type=F32)


def state_body(k_ref, v_ref, kact_ref, state_ref):
    k_act = silu(k_ref[...])
    kact_ref[...] = k_act
    both = contract(k_act, v_ref[...], ((0,), (0,))).astype(BF16)
    for head in range(2):
        square = both[head * DH : (head + 1) * DH, head * DH : (head + 1) * DH]
        for part in range(2):
            column = (2 * head + part) * DH
            state_ref[:, column : column + DH] = square[part * 64 : (part + 1) * 64]


def span_state(key_in, value):
    tokens, width = key_in.shape
    column = pl.BlockSpec((tokens, 2 * DH), lambda h: (0, h))
    return pl.pallas_call(
        state_body,
        grid=(width // (2 * DH),),
        in_specs=[column, column],
        out_specs=[column, pl.BlockSpec((64, 4 * DH), lambda h: (0, h))],
        out_shape=[
            jax.ShapeDtypeStruct((tokens, width), BF16),
            jax.ShapeDtypeStruct((64, 2 * width), BF16),
        ],
        name="span_state",
    )(key_in, value)


def local_body(q_ref, kact_ref, v_ref, qact_ref, local_ref):
    q_act = silu(q_ref[...])
    qact_ref[...] = q_act
    tokens = q_act.shape[0]
    rows = lax.broadcasted_iota(jnp.int32, (CHUNK, CHUNK), 0)
    cols = lax.broadcasted_iota(jnp.int32, (CHUNK, CHUNK), 1)
    running = None
    for start in range(0, tokens, CHUNK):
        q_part = q_act[start : start + CHUNK]
        k_part = kact_ref[start : start + CHUNK, :]
        v_part = v_ref[start : start + CHUNK, :]
        scores = contract(q_part, k_part, ((1,), (1,)))
        scores = jnp.where(rows >= cols, scores, 0.0).astype(BF16)
        inner = contract(scores, v_part, ((1,), (0,)))
        if running is not None:
            inner = inner + contract(q_part, running.astype(BF16), ((1,), (0,)))
        local_ref[start : start + CHUNK, :] = inner
        if start + CHUNK < tokens:
            update = contract(k_part, v_part, ((0,), (0,)))
            running = update if running is None else running + update


def local_attention(query, k_act, value, first, heads):
    tokens, width = query.shape[0], heads * DH
    source = pl.BlockSpec((tokens, DH), lambda h: (0, h + first))
    column = pl.BlockSpec((tokens, DH), lambda h: (0, h))
    return pl.pallas_call(
        local_body,
        grid=(heads,),
        in_specs=[source, source, source],
        out_specs=[column, column],
        out_shape=[
            jax.ShapeDtypeStruct((tokens, width), BF16),
            jax.ShapeDtypeStruct((tokens, width), F32),
        ],
        name="local_attention",
    )(query, k_act, value)


def message_body(tab_ref, state_ref, z1, z2, z3, *outs):
    pieces = [piece[...].astype(F32) for piece in (z1, z2, z3)]
    zero = jnp.zeros_like(pieces[0])
    lower = zero
    for index, piece in enumerate(pieces):
        lower = lower + jnp.where(tab_ref[8 + index] > 0, piece, zero)
    first_core = tab_ref[14] == 0
    through = jnp.where(first_core, zero, lower)
    total = state_ref[...].astype(F32)
    total = total + jnp.where(first_core, pieces[0] + pieces[1] + pieces[2], zero)
    for index, out in enumerate(outs):
        out[...] = (through + jnp.where(tab_ref[11 + index] > 0, total, zero)).astype(BF16)


def messages(table, state, pieces):
    return pl.pallas_call(
        message_body,
        in_specs=[pl.BlockSpec(memory_space=pltpu.SMEM)]
        + [pl.BlockSpec(memory_space=pltpu.VMEM)] * 4,
        out_specs=[pl.BlockSpec(memory_space=pltpu.VMEM)] * 3,
        out_shape=[jax.ShapeDtypeStruct(state.shape, BF16)] * 3,
        name="messages",
    )(table, state, *pieces)


def norm_body(
    tab_ref, q_ref, local_ref, gain_ref, z1, z2, z3, x1, x2, x3, out_ref
):
    prefix = x1[...].astype(F32) + x2[...].astype(F32) + x3[...].astype(F32)
    for index, piece in enumerate((z1, z2, z3)):
        prefix = prefix + jnp.where(tab_ref[8 + index] > 0, piece[...].astype(F32), 0.0)
    prefix = prefix.astype(BF16)
    zero = jnp.zeros((64, DH), BF16)
    strips = [prefix[:, index * DH : (index + 1) * DH] for index in range(4)]
    prefix = jnp.concatenate(
        [jnp.concatenate([strip, zero], axis=1) for strip in strips[:2]]
        + [jnp.concatenate([zero, strip], axis=1) for strip in strips[2:]],
        axis=0,
    )
    head = lax.broadcasted_iota(jnp.int32, (2 * DH, 2 * DH), 0) // DH
    other = lax.broadcasted_iota(jnp.int32, (2 * DH, 2 * DH), 1) // DH
    average = jnp.where(head == other, 1.0 / DH, 0.0).astype(BF16)
    gain = gain_ref[...]
    for place in range(8):
        source = pl.ds(pl.multiple_of(tab_ref[place] * 128, 128), 128)
        attended = local_ref[source, :] + contract(q_ref[source, :], prefix, ((1,), (0,)))
        meansq = contract((attended * attended).astype(BF16), average, ((1,), (0,)))
        normed = (attended * lax.rsqrt(meansq + 1e-06) * gain).astype(BF16)
        out_ref[place * 128 : (place + 1) * 128, :] = normed


def norm(table, half, first, gain, z_pieces, x_pieces):
    tokens, width = half[0].shape
    skip = first * DH // (2 * DH)
    pair = pl.BlockSpec((tokens, 2 * DH), lambda h, t: (0, h))
    last = pl.BlockSpec((64, 4 * DH), lambda h, t: (0, h + skip))
    square = pl.BlockSpec((64, 4 * DH), lambda h, t: (0, h + skip))
    return pl.pallas_call(
        norm_body,
        grid_spec=pltpu.PrefetchScalarGridSpec(
            num_scalar_prefetch=1,
            grid=(width // (2 * DH),),
            in_specs=[pair, pair, pl.BlockSpec((1, 2 * DH), lambda h, t: (0, h + skip))]
            + [last] * 3
            + [square] * 3,
            out_specs=pair,
        ),
        out_shape=jax.ShapeDtypeStruct((tokens, width), BF16),
        name="norm",
    )(table, *half, gain, *z_pieces, *x_pieces)


def project_body(core_ref, *refs):
    tokens, (a_first, a_second, b_first, b_second), outs = refs[:4], refs[4:8], refs[8:]
    step = pl.program_id(0)
    rows = outs[0].shape[0]
    first_core = core_ref[0] == 0
    pairs = ((a_first, a_second), (a_first, b_first), (b_first, b_second))
    for index, (upper, lower) in enumerate(pairs):

        @pl.when(step == index)
        def _(upper=upper, lower=lower):
            joined = jnp.concatenate([t_ref[...] for t_ref in tokens], axis=1)
            weights = jnp.concatenate([upper[...], lower[...]], axis=0)
            total = contract(joined, weights, ((1,), (1,)))
            far, right, left, own = (
                total[place * rows : (place + 1) * rows].astype(BF16) for place in range(4)
            )
            for out, block in zip(
                outs,
                (jnp.where(first_core, left, right), far, jnp.where(first_core, right, left), own),
            ):
                out[...] = block


def project(core, tokens, weights):
    rows = tokens[0].shape[0]
    first, second = weights
    tile, depth = first.shape[0] // 3, first.shape[1]
    columns = 6 * tile

    def piece(place):
        return pl.BlockSpec((tile, depth), lambda g, t: (place(g), 0))

    whole = pl.BlockSpec(memory_space=pltpu.VMEM)
    return pl.pallas_call(
        project_body,
        grid_spec=pltpu.PrefetchScalarGridSpec(
            num_scalar_prefetch=1,
            grid=(3,),
            in_specs=[whole] * 4
            + [
                piece(lambda g: jnp.minimum(2 * g, 2)),
                piece(lambda g: 1),
                piece(lambda g: jnp.maximum(g - 1, 0)),
                piece(lambda g: 2),
            ],
            out_specs=[pl.BlockSpec((rows // 4, 2 * tile), lambda g, t: (0, g))] * 4,
        ),
        out_shape=[jax.ShapeDtypeStruct((rows // 4, columns), BF16)] * 4,
        compiler_params=pltpu.CompilerParams(vmem_limit_bytes=24 * 1024 * 1024),
        name="project",
    )(core, *tokens, first, first, second, second)


def finish_body(layout, tab_ref, res_ref, *refs):
    out_ref = refs[-1]
    kept, got = refs[: len(refs) // 2], refs[len(refs) // 2 : -1]
    first_core = tab_ref[16] == 0
    groups = []
    for keep, receive in zip(kept, got):
        mine, theirs = keep[...], receive[...].astype(F32)
        groups.append((jnp.where(first_core, mine, theirs), jnp.where(first_core, theirs, mine)))
    for place, ((c0, o0), (c1, o1)) in enumerate(layout):
        both = jnp.concatenate(
            [groups[c0][0][:, o0 : o0 + 192], groups[c1][1][:, o1 : o1 + 192]], axis=1
        )
        target = pl.ds(pl.multiple_of(tab_ref[place] * 384, 128), 384)
        out_ref[:, target] = (both + res_ref[:, target].astype(F32)).astype(BF16)


def finish(layout, table, residual, kept, got):
    return pl.pallas_call(
        functools.partial(finish_body, layout),
        in_specs=[pl.BlockSpec(memory_space=pltpu.SMEM)]
        + [pl.BlockSpec(memory_space=pltpu.VMEM)] * (1 + len(kept) + len(got)),
        out_specs=pl.BlockSpec(memory_space=pltpu.VMEM),
        out_shape=jax.ShapeDtypeStruct(residual.shape, BF16),
        compiler_params=pltpu.CompilerParams(vmem_limit_bytes=40 * 1024 * 1024),
        name="finish",
    )(table, residual, *kept, *got)


def fetch(array, axis, offset):
    return lax.ppermute(array, axis, [((i + offset) % 4, i) for i in range(4)])


def fetch_mixed(array, level, offset):
    pairs = []
    for x in range(4):
        for z in range(4):
            for c in range(2):
                if (level == 1) == (c == 0):
                    source = (x, (z + offset) % 4, c)
                else:
                    source = ((x + offset) % 4, z, c)
                pairs.append(((source[0] * 4 + source[1]) * 2 + c, (x * 4 + z) * 2 + c))
    return lax.ppermute(array, ("x", "z", "c"), pairs)


def swap(array):
    return lax.ppermute(array, "c", [(0, 1), (1, 0)])


def push(array, hops):
    pairs = []
    for y in range(4):
        pairs.append((y * 2, (y + hops) % 4 * 2))
        pairs.append((y * 2 + 1, (y - hops) % 4 * 2 + 1))
    return lax.ppermute(array, ("y", "c"), pairs)


def add(left, right):
    return (left.astype(F32) + right.astype(F32)).astype(BF16)


def settle_chunk(parts, c):
    def rows(which):
        total = 0.0
        for part in parts:
            total = total + lax.dynamic_slice_in_dim(part, which * 128, 128).astype(F32)
        return total

    return rows(c), swap(rows(1 - c).astype(BF16))


def per_device(query, key_in, value, head_gain, out_weight, residual):
    x, z, y, c = (lax.axis_index(name) for name in ("x", "z", "y", "c"))
    near, away = jnp.where(c == 0, z, x), jnp.where(c == 0, x, z)
    blocks = [(y + offset) % 4 * 2 + core for offset in YREL for core in (0, 1)]
    flags = [(near + offset) % 4 < near for offset in REL[1:]]
    flags += [away < (away - offset) % 4 for offset in REL[1:]]
    table = jnp.stack([jnp.asarray(entry, jnp.int32) for entry in blocks + flags + [c]])

    turned = out_weight.T
    half = turned.shape[0] // 2
    keep = lax.dynamic_slice_in_dim(turned, c * half, half)
    give = lax.dynamic_slice_in_dim(turned, (1 - c) * half, half)
    k_act, state = span_state(after(key_in, keep, give), value)
    base = jnp.concatenate([keep, after(swap(give), state)], axis=1)
    level1 = [fetch_mixed(state, 1, offset) for offset in REL[1:]]
    plus, minus = fetch_mixed(base, 1, 1), fetch_mixed(base, 1, 3)

    width = query.shape[1] // 2
    heads = width // DH
    early = local_attention(query, k_act, value, 0, heads)
    level1 = [after(piece, early[0], plus, minus) for piece in level1]
    sent = messages(table, state, level1)
    level2 = [fetch_mixed(piece, 2, offset) for piece, offset in zip(sent, REL[1:])]
    late = local_attention(after(query, sent[0]), k_act, value, heads, heads)
    level2 = [after(piece, late[0]) for piece in level2]
    g0a = jnp.concatenate([base, plus], axis=0)
    g0a = after(g0a, *level2)
    far = fetch_mixed(after(base, *level2), 1, 2)
    g1a, g3a = fetch_mixed(g0a, 2, 1), fetch_mixed(g0a, 2, 3)
    g0b = jnp.concatenate([minus, far], axis=0)

    gain = head_gain.reshape(1, -1)
    norm_a = norm(table, early, 0, gain, level1, level2)
    swap_a = swap(norm_a)
    norm_b = norm(after(table, norm_a), late, heads, gain, level1, level2)
    swap_b = swap(norm_b)
    core = c.astype(jnp.int32).reshape(1)
    ready = after(g0b, g1a, g3a)
    g1b, g3b = fetch_mixed(ready, 2, 1), fetch_mixed(ready, 2, 3)

    def columns(weights, *others):
        return project(core, [after(norm_a, *others), norm_b, swap_a, swap_b], weights)

    first = columns([g1a, g3a], norm_b)
    second = columns([g0a, g0b], first[0])
    first1 = push(first[0], 1)
    second1 = push(after(second[0], first1), 1)
    first2 = push(after(add(first1, first[1]), second[0]), 1)
    g2 = [
        fetch_mixed(after(g1a, g1b, g3b, second[0], first1), 2, 1),
        fetch_mixed(after(g3b, g1b, second[0], first1), 2, 3),
    ]
    second2 = push(add(second1, second[1]), 1)
    third = columns([g1b, g3b], second[0], first1)
    third1 = push(after(third[0], first2), 1)
    first3 = push(add(first2, first[2]), 1)
    second3 = push(add(second2, second[2]), 1)
    third2 = push(add(third1, third[1]), 1)
    third3 = push(add(third2, third[2]), 1)
    fourth = columns(g2, third[0], first2, second2)
    chunks = (
        (first[3], first3),
        (second[3], second3),
        (third[3], third3),
        (fourth[3], push(fourth[1], 2), push(fourth[2], 1), push(fourth[0], 3)),
    )
    settled = [settle_chunk(parts, c) for parts in chunks]
    spot = (
        ((1, 0), (1, 1), (1, 2), (1, 3)),
        ((0, 0), (0, 1), (2, 0), (2, 1)),
        ((0, 2), (0, 3), (2, 2), (2, 3)),
        ((3, 0), (3, 1), (3, 2), (3, 3)),
    )
    layout, shards = [], []
    for i, x_off in enumerate(REL):
        for j, z_off in enumerate(REL):
            layout.append(
                tuple((chunk, part * half) for chunk, part in (spot[i][j], spot[j][i]))
            )
            shards.append((x + x_off) % 4 * 4 + (z + z_off) % 4)
    shard_table = jnp.stack([jnp.asarray(entry, jnp.int32) for entry in shards + [c]])
    kept, got = zip(*settled)
    return finish(tuple(layout), shard_table, residual, kept, got)


def solution(mesh):
    torus = Mesh(mesh.devices.reshape(4, 4, 4, 2), ("x", "z", "y", "c"))
    seq, hx = ("x", "z"), ("y", "c")
    return jax.shard_map(
        per_device,
        mesh=torus,
        in_specs=(P(seq, hx), P(seq, hx), P(seq, hx), P(hx), P(hx, seq), P(seq + hx, None)),
        out_specs=P(seq + hx, None),
        check_vma=False,
    )
```

```python
import functools

import jax
import jax.numpy as jnp
from jax import lax
from jax.experimental import pallas as pl
from jax.experimental.pallas import tpu as pltpu
from jax.sharding import Mesh, PartitionSpec as P

DH = 128
F32 = jnp.float32
BF16 = jnp.bfloat16
REL = (0, 1, 3, 2)
YREL = (2, 1, 3, 0)
CHUNK = 256


def silu(block):
    wide = block.astype(F32)
    return (0.5 * wide * (1.0 + jnp.tanh(0.5 * wide))).astype(BF16)


def after(value, *others):
    return lax.optimization_barrier((value, *others))[0]


def contract(left, right, dims):
    return lax.dot_general(left, right, (dims, ((), ())), preferred_element_type=F32)


def state_body(k_ref, v_ref, kact_ref, state_ref):
    k_act = silu(k_ref[...])
    kact_ref[...] = k_act
    both = contract(k_act, v_ref[...], ((0,), (0,))).astype(BF16)
    for head in range(2):
        square = both[head * DH : (head + 1) * DH, head * DH : (head + 1) * DH]
        for part in range(2):
            column = (2 * head + part) * DH
            state_ref[:, column : column + DH] = square[part * 64 : (part + 1) * 64]


def span_state(key_in, value):
    tokens, width = key_in.shape
    column = pl.BlockSpec((tokens, 2 * DH), lambda h: (0, h))
    return pl.pallas_call(
        state_body,
        grid=(width // (2 * DH),),
        in_specs=[column, column],
        out_specs=[column, pl.BlockSpec((64, 4 * DH), lambda h: (0, h))],
        out_shape=[
            jax.ShapeDtypeStruct((tokens, width), BF16),
            jax.ShapeDtypeStruct((64, 2 * width), BF16),
        ],
        name="span_state",
    )(key_in, value)


def local_body(q_ref, kact_ref, v_ref, qact_ref, local_ref):
    q_act = silu(q_ref[...])
    qact_ref[...] = q_act
    tokens = q_act.shape[0]
    rows = lax.broadcasted_iota(jnp.int32, (CHUNK, CHUNK), 0)
    cols = lax.broadcasted_iota(jnp.int32, (CHUNK, CHUNK), 1)
    running = None
    for start in range(0, tokens, CHUNK):
        q_part = q_act[start : start + CHUNK]
        k_part = kact_ref[start : start + CHUNK, :]
        v_part = v_ref[start : start + CHUNK, :]
        scores = contract(q_part, k_part, ((1,), (1,)))
        scores = jnp.where(rows >= cols, scores, 0.0).astype(BF16)
        inner = contract(scores, v_part, ((1,), (0,)))
        if running is not None:
            inner = inner + contract(q_part, running.astype(BF16), ((1,), (0,)))
        local_ref[start : start + CHUNK, :] = inner
        if start + CHUNK < tokens:
            update = contract(k_part, v_part, ((0,), (0,)))
            running = update if running is None else running + update


def local_attention(query, k_act, value, first, heads):
    tokens, width = query.shape[0], heads * DH
    source = pl.BlockSpec((tokens, DH), lambda h: (0, h + first))
    column = pl.BlockSpec((tokens, DH), lambda h: (0, h))
    return pl.pallas_call(
        local_body,
        grid=(heads,),
        in_specs=[source, source, source],
        out_specs=[column, column],
        out_shape=[
            jax.ShapeDtypeStruct((tokens, width), BF16),
            jax.ShapeDtypeStruct((tokens, width), F32),
        ],
        name="local_attention",
    )(query, k_act, value)


def message_body(tab_ref, state_ref, z1, z2, z3, *outs):
    pieces = [piece[...].astype(F32) for piece in (z1, z2, z3)]
    zero = jnp.zeros_like(pieces[0])
    lower = zero
    for index, piece in enumerate(pieces):
        lower = lower + jnp.where(tab_ref[8 + index] > 0, piece, zero)
    first_core = tab_ref[14] == 0
    through = jnp.where(first_core, zero, lower)
    total = state_ref[...].astype(F32)
    total = total + jnp.where(first_core, pieces[0] + pieces[1] + pieces[2], zero)
    for index, out in enumerate(outs):
        out[...] = (through + jnp.where(tab_ref[11 + index] > 0, total, zero)).astype(BF16)


def messages(table, state, pieces):
    return pl.pallas_call(
        message_body,
        in_specs=[pl.BlockSpec(memory_space=pltpu.SMEM)]
        + [pl.BlockSpec(memory_space=pltpu.VMEM)] * 4,
        out_specs=[pl.BlockSpec(memory_space=pltpu.VMEM)] * 3,
        out_shape=[jax.ShapeDtypeStruct(state.shape, BF16)] * 3,
        name="messages",
    )(table, state, *pieces)


def norm_body(
    tab_ref, q_ref, local_ref, gain_ref, z1, z2, z3, x1, x2, x3, out_ref
):
    prefix = x1[...].astype(F32) + x2[...].astype(F32) + x3[...].astype(F32)
    for index, piece in enumerate((z1, z2, z3)):
        prefix = prefix + jnp.where(tab_ref[8 + index] > 0, piece[...].astype(F32), 0.0)
    prefix = prefix.astype(BF16)
    zero = jnp.zeros((64, DH), BF16)
    strips = [prefix[:, index * DH : (index + 1) * DH] for index in range(4)]
    prefix = jnp.concatenate(
        [jnp.concatenate([strip, zero], axis=1) for strip in strips[:2]]
        + [jnp.concatenate([zero, strip], axis=1) for strip in strips[2:]],
        axis=0,
    )
    head = lax.broadcasted_iota(jnp.int32, (2 * DH, 2 * DH), 0) // DH
    other = lax.broadcasted_iota(jnp.int32, (2 * DH, 2 * DH), 1) // DH
    average = jnp.where(head == other, 1.0 / DH, 0.0).astype(BF16)
    gain = gain_ref[...]
    for place in range(8):
        source = pl.ds(pl.multiple_of(tab_ref[place] * 128, 128), 128)
        attended = local_ref[source, :] + contract(q_ref[source, :], prefix, ((1,), (0,)))
        meansq = contract((attended * attended).astype(BF16), average, ((1,), (0,)))
        normed = (attended * lax.rsqrt(meansq + 1e-06) * gain).astype(BF16)
        out_ref[place * 128 : (place + 1) * 128, :] = normed


def norm(table, half, first, gain, z_pieces, x_pieces):
    tokens, width = half[0].shape
    skip = first * DH // (2 * DH)
    pair = pl.BlockSpec((tokens, 2 * DH), lambda h, t: (0, h))
    last = pl.BlockSpec((64, 4 * DH), lambda h, t: (0, h + skip))
    square = pl.BlockSpec((64, 4 * DH), lambda h, t: (0, h + skip))
    return pl.pallas_call(
        norm_body,
        grid_spec=pltpu.PrefetchScalarGridSpec(
            num_scalar_prefetch=1,
            grid=(width // (2 * DH),),
            in_specs=[pair, pair, pl.BlockSpec((1, 2 * DH), lambda h, t: (0, h + skip))]
            + [last] * 3
            + [square] * 3,
            out_specs=pair,
        ),
        out_shape=jax.ShapeDtypeStruct((tokens, width), BF16),
        name="norm",
    )(table, *half, gain, *z_pieces, *x_pieces)


def project_body(core_ref, *refs):
    tokens, (a_first, a_second, b_first, b_second), outs = refs[:4], refs[4:8], refs[8:]
    step = pl.program_id(0)
    rows = outs[0].shape[0]
    first_core = core_ref[0] == 0
    pairs = ((a_first, a_second), (a_first, b_first), (b_first, b_second))
    for index, (upper, lower) in enumerate(pairs):

        @pl.when(step == index)
        def _(upper=upper, lower=lower):
            joined = jnp.concatenate([t_ref[...] for t_ref in tokens], axis=1)
            weights = jnp.concatenate([upper[...], lower[...]], axis=0)
            total = contract(joined, weights, ((1,), (1,)))
            far, right, left, own = (
                total[place * rows : (place + 1) * rows].astype(BF16) for place in range(4)
            )
            for out, block in zip(
                outs,
                (jnp.where(first_core, left, right), far, jnp.where(first_core, right, left), own),
            ):
                out[...] = block


def project(core, tokens, weights):
    rows = tokens[0].shape[0]
    first, second = weights
    tile, depth = first.shape[0] // 3, first.shape[1]
    columns = 6 * tile

    def piece(place):
        return pl.BlockSpec((tile, depth), lambda g, t: (place(g), 0))

    whole = pl.BlockSpec(memory_space=pltpu.VMEM)
    return pl.pallas_call(
        project_body,
        grid_spec=pltpu.PrefetchScalarGridSpec(
            num_scalar_prefetch=1,
            grid=(3,),
            in_specs=[whole] * 4
            + [
                piece(lambda g: jnp.minimum(2 * g, 2)),
                piece(lambda g: 1),
                piece(lambda g: jnp.maximum(g - 1, 0)),
                piece(lambda g: 2),
            ],
            out_specs=[pl.BlockSpec((rows // 4, 2 * tile), lambda g, t: (0, g))] * 4,
        ),
        out_shape=[jax.ShapeDtypeStruct((rows // 4, columns), BF16)] * 4,
        compiler_params=pltpu.CompilerParams(vmem_limit_bytes=24 * 1024 * 1024),
        name="project",
    )(core, *tokens, first, first, second, second)


def finish_body(layout, tab_ref, res_ref, *refs):
    out_ref = refs[-1]
    kept, got = refs[: len(refs) // 2], refs[len(refs) // 2 : -1]
    first_core = tab_ref[16] == 0
    groups = []
    for keep, receive in zip(kept, got):
        mine, theirs = keep[...], receive[...].astype(F32)
        groups.append((jnp.where(first_core, mine, theirs), jnp.where(first_core, theirs, mine)))
    for place, ((c0, o0), (c1, o1)) in enumerate(layout):
        both = jnp.concatenate(
            [groups[c0][0][:, o0 : o0 + 192], groups[c1][1][:, o1 : o1 + 192]], axis=1
        )
        target = pl.ds(pl.multiple_of(tab_ref[place] * 384, 128), 384)
        out_ref[:, target] = (both + res_ref[:, target].astype(F32)).astype(BF16)


def finish(layout, table, residual, kept, got):
    return pl.pallas_call(
        functools.partial(finish_body, layout),
        in_specs=[pl.BlockSpec(memory_space=pltpu.SMEM)]
        + [pl.BlockSpec(memory_space=pltpu.VMEM)] * (1 + len(kept) + len(got)),
        out_specs=pl.BlockSpec(memory_space=pltpu.VMEM),
        out_shape=jax.ShapeDtypeStruct(residual.shape, BF16),
        compiler_params=pltpu.CompilerParams(vmem_limit_bytes=40 * 1024 * 1024),
        name="finish",
    )(table, residual, *kept, *got)


def fetch(array, axis, offset):
    return lax.ppermute(array, axis, [((i + offset) % 4, i) for i in range(4)])


def fetch_mixed(array, level, offset):
    pairs = []
    for x in range(4):
        for z in range(4):
            for c in range(2):
                if (level == 1) == (c == 0):
                    source = (x, (z + offset) % 4, c)
                else:
                    source = ((x + offset) % 4, z, c)
                pairs.append(((source[0] * 4 + source[1]) * 2 + c, (x * 4 + z) * 2 + c))
    return lax.ppermute(array, ("x", "z", "c"), pairs)


def swap(array):
    return lax.ppermute(array, "c", [(0, 1), (1, 0)])


def push(array, hops):
    pairs = []
    for y in range(4):
        pairs.append((y * 2, (y + hops) % 4 * 2))
        pairs.append((y * 2 + 1, (y - hops) % 4 * 2 + 1))
    return lax.ppermute(array, ("y", "c"), pairs)


def add(left, right):
    return (left.astype(F32) + right.astype(F32)).astype(BF16)


def settle_chunk(parts, c):
    def rows(which):
        total = 0.0
        for part in parts:
            total = total + lax.dynamic_slice_in_dim(part, which * 128, 128).astype(F32)
        return total

    return rows(c), swap(rows(1 - c).astype(BF16))


def per_device(query, key_in, value, head_gain, out_weight, residual):
    x, z, y, c = (lax.axis_index(name) for name in ("x", "z", "y", "c"))
    near, away = jnp.where(c == 0, z, x), jnp.where(c == 0, x, z)
    blocks = [(y + offset) % 4 * 2 + core for offset in YREL for core in (0, 1)]
    flags = [(near + offset) % 4 < near for offset in REL[1:]]
    flags += [away < (away - offset) % 4 for offset in REL[1:]]
    table = jnp.stack([jnp.asarray(entry, jnp.int32) for entry in blocks + flags + [c]])

    turned = out_weight.T
    half = turned.shape[0] // 2
    keep = lax.dynamic_slice_in_dim(turned, c * half, half)
    give = lax.dynamic_slice_in_dim(turned, (1 - c) * half, half)
    k_act, state = span_state(after(key_in, keep, give), value)
    base = jnp.concatenate([keep, after(swap(give), state)], axis=1)
    level1 = [fetch_mixed(state, 1, offset) for offset in REL[1:]]
    plus, minus = fetch_mixed(base, 1, 1), fetch_mixed(base, 1, 3)

    width = query.shape[1] // 2
    heads = width // DH
    early = local_attention(query, k_act, value, 0, heads)
    level1 = [after(piece, early[0], plus, minus) for piece in level1]
    sent = messages(table, state, level1)
    level2 = [fetch_mixed(piece, 2, offset) for piece, offset in zip(sent, REL[1:])]
    late = local_attention(after(query, sent[0]), k_act, value, heads, heads)
    level2 = [after(piece, late[0]) for piece in level2]
    g0a = jnp.concatenate([base, plus], axis=0)
    g0a = after(g0a, *level2)
    upper = fetch_mixed(after(plus[: half // 2], *level2), 1, 1)
    lower = fetch_mixed(after(minus[half // 2 :], *level2), 1, 3)
    g1a, g3a = fetch_mixed(g0a, 2, 1), fetch_mixed(g0a, 2, 3)
    g0b = jnp.concatenate([minus, upper, lower], axis=0)

    gain = head_gain.reshape(1, -1)
    norm_a = norm(table, early, 0, gain, level1, level2)
    swap_a = swap(norm_a)
    norm_b = norm(after(table, norm_a), late, heads, gain, level1, level2)
    swap_b = swap(norm_b)
    core = c.astype(jnp.int32).reshape(1)
    ready = after(g0b, g1a, g3a)
    g1b, g3b = fetch_mixed(ready, 2, 1), fetch_mixed(ready, 2, 3)

    def columns(weights, *others):
        return project(core, [after(norm_a, *others), norm_b, swap_a, swap_b], weights)

    first = columns([g1a, g3a], norm_b)
    second = columns([g0a, g0b], first[0])
    first1 = push(first[0], 1)
    second1 = push(after(second[0], first1), 1)
    first2 = push(after(add(first1, first[1]), second[0]), 1)
    g2 = [
        fetch_mixed(after(g1a, g1b, g3b, second[0], first1), 2, 1),
        fetch_mixed(after(g3b, g1b, second[0], first1), 2, 3),
    ]
    second2 = push(add(second1, second[1]), 1)
    third = columns([g1b, g3b], second[0], first1)
    third1 = push(after(third[0], first2), 1)
    first3 = push(add(first2, first[2]), 1)
    second3 = push(add(second2, second[2]), 1)
    third2 = push(add(third1, third[1]), 1)
    third3 = push(add(third2, third[2]), 1)
    fourth = columns(g2, third[0], first2, second2)
    chunks = (
        (first[3], first3),
        (second[3], second3),
        (third[3], third3),
        (fourth[3], push(fourth[1], 2), push(fourth[2], 1), push(fourth[0], 3)),
    )
    settled = [settle_chunk(parts, c) for parts in chunks]
    spot = (
        ((1, 0), (1, 1), (1, 2), (1, 3)),
        ((0, 0), (0, 1), (2, 0), (2, 1)),
        ((0, 2), (0, 3), (2, 2), (2, 3)),
        ((3, 0), (3, 1), (3, 2), (3, 3)),
    )
    layout, shards = [], []
    for i, x_off in enumerate(REL):
        for j, z_off in enumerate(REL):
            layout.append(
                tuple((chunk, part * half) for chunk, part in (spot[i][j], spot[j][i]))
            )
            shards.append((x + x_off) % 4 * 4 + (z + z_off) % 4)
    shard_table = jnp.stack([jnp.asarray(entry, jnp.int32) for entry in shards + [c]])
    kept, got = zip(*settled)
    return finish(tuple(layout), shard_table, residual, kept, got)


def solution(mesh):
    torus = Mesh(mesh.devices.reshape(4, 4, 4, 2), ("x", "z", "y", "c"))
    seq, hx = ("x", "z"), ("y", "c")
    return jax.shard_map(
        per_device,
        mesh=torus,
        in_specs=(P(seq, hx), P(seq, hx), P(seq, hx), P(hx), P(hx, seq), P(seq + hx, None)),
        out_specs=P(seq + hx, None),
        check_vma=False,
    )
```
